256 devices in a mesh: ctx: 8 (over y_hi, x), ch: 32 (over y_lo, z, core).
Axes of the slice: x: 4, y: 4 (y_hi: 2, y_lo: 2; y = y_hi * 2 + y_lo), z: 8, core: 2. Of those that a mesh axis runs over, the one named last changes fastest.
Arguments:
- conv_input: bfloat16 [8192, 4096], P('ch', 'ctx'), may hold values from -0.03125 to 0.03125
- output_grad: bfloat16 [8192, 4096], P('ch', 'ctx'), may hold values from -6 to 6
- long_filter: bfloat16 [128, 4096], P(None, 'ctx'), may hold values from -0.09375 to 0.09375
Outputs:
- input_grad: bfloat16 [8192, 4096], P('ch', 'ctx')
- filter_grad: float32 [128, 4096], P(None, 'ctx')
The draws below stay inside these ranges and needn't reach their ends.
All inputs are finite; a program needn't handle non-finite values.
Results may differ from the reference program's by a relative error of at most 0.001.
Values may be sent and summed in bfloat16 or wider, within the bound.
No kernel may reach another device: no remote copies, remote signals or barrier semaphores. Data moves between devices by JAX's collectives and lax.ppermute only.
A program may use at most 128 MiB of HBM per device.

```python
import jax
import jax.numpy as jnp

C = 8192
G = 128
TOKENS = 4096
GS = 64


def block_scale(own_key, extent, split, smallest, high):
    loudness, own = 1.0, jax.random.fold_in(own_key, 6)
    for position, blocks in split:
        draws = jnp.exp(jax.random.uniform(jax.random.fold_in(own, position), (blocks,), jnp.float32, smallest / len(split), high / len(split)))
        loudness = loudness * jnp.repeat(draws, extent[position] // blocks).reshape([-1 if axis == position else 1 for axis in range(len(extent))])
    return loudness


def centred(key, dims, spread, bound, pieces=(), dtype=jnp.bfloat16):
    drawn = spread * jax.random.normal(key, dims, jnp.float32)
    if pieces:
        drawn = drawn * block_scale(key, dims, pieces, -0.22, 0.18)
    return jnp.clip(drawn, -bound, bound).astype(dtype)


def setup_inputs(seed: int = 0) -> dict:
    arg_keys = jax.random.split(jax.random.key(seed), 4)
    conv_input = centred(arg_keys[0], (C, TOKENS), ((GS * TOKENS) ** -0.5), 0.03125, ((0, 32), (1, 8)))
    output_grad = centred(arg_keys[1], (C, TOKENS), 1.0, 6.0, ((0, 32), (1, 8)))
    long_filter = centred(arg_keys[2], (G, TOKENS), TOKENS ** -0.5, 0.09375, ((1, 8),))
    return {"conv_input": conv_input, "output_grad": output_grad, "long_filter": long_filter}


def reference(conv_input, output_grad, long_filter):
    fft_length = 2 * TOKENS
    input_freq = jnp.fft.rfft(conv_input.astype(jnp.float32), n=fft_length, axis=1)
    grad_freq = jnp.fft.rfft(output_grad.astype(jnp.float32), n=fft_length, axis=1)
    filter_freq = jnp.fft.rfft(long_filter.astype(jnp.float32), n=fft_length, axis=1)
    channel_freq = jnp.repeat(filter_freq, C // G, axis=0)
    input_grad = jnp.fft.irfft(jnp.conj(channel_freq) * grad_freq, n=fft_length, axis=1)[:, :TOKENS]
    cross_freq = jnp.sum((jnp.conj(input_freq) * grad_freq).reshape(G, C // G, -1), axis=1)
    filter_grad = jnp.fft.irfft(cross_freq, n=fft_length, axis=1)[:, :TOKENS]
    return input_grad.astype(jnp.bfloat16), filter_grad.astype(jnp.float32)
```

```python
import jax
import jax.numpy as jnp
from jax import lax
from jax.experimental import pallas as pl
from jax.experimental.pallas import tpu as pltpu
from jax.sharding import PartitionSpec as P

C = 8192
G = 128
TILE = 256


def roll_left(x, amount):
    lanes = x.shape[1]
    return x if amount == 0 else pltpu.roll(x, lanes - amount, 1)


def gradients_kernel(recv_ref, out_ref, og_ref, cit_ref, table_ref, skew_ref, acc_ref):
    blocks, _, own = recv_ref.shape
    per = 32
    tokens = blocks * own
    tiles = tokens // TILE
    rows = tiles * per

    ci = []
    for a in range(tiles):
        j, lo = (a * TILE) // own, (a * TILE) % own
        og_ref[a * per : (a + 1) * per, :] = recv_ref[j, per : 2 * per, lo : lo + TILE]
        ci.append(recv_ref[j, 0:per, lo : lo + TILE])
    og_ref[rows : 2 * rows, :] = jnp.zeros((rows, TILE), og_ref.dtype)
    cit_ref[...] = jnp.concatenate(ci, axis=0).T

    taps = jnp.concatenate(
        [recv_ref[j, 2 * per : 2 * per + 1, :].astype(jnp.float32) for j in range(blocks)], axis=1
    )
    wide = jnp.broadcast_to(taps, (8, tokens))
    base = pltpu.roll(wide, 0, 1, stride=1, stride_axis=0)
    for t in range(0, 16, 2):
        pair = jnp.concatenate(
            [base if t == 0 else pltpu.roll(base, 8 * t, 1), pltpu.roll(base, 8 * t + 8, 1)], axis=0
        )
        u = 8 * t + lax.broadcasted_iota(jnp.int32, (16, 128), 0)
        first = jnp.where(lax.broadcasted_iota(jnp.int32, (16, 128), 1) >= u, pair[:, 0:128], 0.0)
        pair = jnp.concatenate([first, pair[:, 128:]], axis=1).astype(jnp.bfloat16)
        table_ref[8 * t : 8 * t + 16, :] = pair
        table_ref[128 + 8 * t : 128 + 8 * t + 16, 128:] = pair[:, : tokens - 128]
        table_ref[128 + 8 * t : 128 + 8 * t + 16, 0:128] = jnp.zeros((16, 128), jnp.bfloat16)

    for d in range(tiles):
        depth = rows if d < tiles // 2 else rows // 2
        cross = jnp.dot(
            cit_ref[:, 0:depth],
            og_ref[d * per : d * per + depth, :],
            preferred_element_type=jnp.float32,
        )
        if d == 0:
            u = lax.broadcasted_iota(jnp.int32, (TILE, TILE), 0)
            v = lax.broadcasted_iota(jnp.int32, (TILE, TILE), 1)
            cross = jnp.where(v >= u, cross, 0.0)
        upper, lower = cross[0:128, :], cross[128:256, :]
        at = d * TILE
        skew_ref[:, at : at + 128] = upper[:, 0:128] + lower[:, 128:256]
        skew_ref[:, at + 128 : at + 256] = upper[:, 128:256]
        if d > 0:
            skew_ref[:, at - 128 : at] = skew_ref[:, at - 128 : at] + lower[:, 0:128]
    folded = skew_ref[0:8, :]
    for t in range(1, 16):
        folded = folded + roll_left(skew_ref[8 * t : 8 * t + 8, :], 8 * t)
    lags = folded[0:1, :]
    for r in range(1, 8):
        lags = lags + roll_left(folded[r : r + 1, :], r)
    high = lags.astype(jnp.bfloat16).astype(jnp.float32)
    low = lags - high
    row = lax.broadcasted_iota(jnp.int32, (8, own), 0)
    for j in range(blocks):
        part = slice(j * own, (j + 1) * own)
        packed = jnp.where(row == 0, high[:, part], jnp.where(row == 1, low[:, part], 0.0))
        out_ref[j, per : per + 8, :] = packed.astype(jnp.bfloat16)

    for d in range(tiles):
        live = rows - d * per
        term = lax.dot_general(
            og_ref[d * per : rows, :],
            table_ref[:, d * TILE : (d + 1) * TILE],
            (((1,), (1,)), ((), ())),
            preferred_element_type=jnp.float32,
        )
        if d == 0:
            acc_ref[...] = term
        else:
            acc_ref[0:live, :] = acc_ref[0:live, :] + term
    for a in range(tiles):
        j, lo = (a * TILE) // own, (a * TILE) % own
        out_ref[j, 0:per, lo : lo + TILE] = acc_ref[a * per : (a + 1) * per, :].astype(jnp.bfloat16)


def gradients(recv):
    blocks, _, own = recv.shape
    tokens = blocks * own
    rows = tokens // TILE * 32
    return pl.pallas_call(
        gradients_kernel,
        out_shape=jax.ShapeDtypeStruct((blocks, 40, own), jnp.bfloat16),
        in_specs=[pl.BlockSpec(memory_space=pltpu.VMEM)],
        out_specs=pl.BlockSpec(memory_space=pltpu.VMEM),
        scratch_shapes=[
            pltpu.VMEM((2 * rows, TILE), jnp.bfloat16),
            pltpu.VMEM((TILE, rows), jnp.bfloat16),
            pltpu.VMEM((TILE, tokens), jnp.bfloat16),
            pltpu.VMEM((128, tokens), jnp.float32),
            pltpu.VMEM((rows, TILE), jnp.float32),
        ],
        name="gradients",
    )(recv)


def per_device(conv_input, output_grad, long_filter):
    channels, own = conv_input.shape
    cycle = lax.axis_size("ctx")
    share = channels // cycle
    groups_here = channels // (C // G)
    first_group = lax.axis_index("ch") * groups_here
    taps = lax.dynamic_slice_in_dim(long_filter, first_group, groups_here, 0)
    taps = jnp.repeat(taps, cycle // groups_here, axis=0)[:, None, :]
    send = jnp.concatenate(
        [
            conv_input.reshape(cycle, share, own),
            output_grad.reshape(cycle, share, own),
            taps,
        ],
        axis=1,
    )
    recv = lax.all_to_all(send, "ctx", 0, 0, tiled=True)
    back = lax.all_to_all(gradients(recv), "ctx", 0, 0, tiled=True)
    input_grad = back[:, :share, :].reshape(channels, own)
    parts = back[:, share : share + 2, :].astype(jnp.float32)
    owned = jnp.sum(parts.reshape(groups_here, -1, own), axis=1)
    peers = lax.axis_size("ch")
    everyone = lax.all_to_all(
        jnp.broadcast_to(owned[None], (peers, groups_here, own)), "ch", 0, 0, tiled=True
    )
    return input_grad, everyone.reshape(G, own)


def solution(mesh):
    in_specs = (P("ch", "ctx"), P("ch", "ctx"), P(None, "ctx"))
    out_specs = (P("ch", "ctx"), P(None, "ctx"))
    return jax.shard_map(
        per_device, mesh=mesh, in_specs=in_specs, out_specs=out_specs, check_vma=False
    )
```

```python
import jax
import jax.numpy as jnp
from jax import lax
from jax.experimental import pallas as pl
from jax.experimental.pallas import tpu as pltpu
from jax.sharding import PartitionSpec as P

C = 8192
G = 128
TILE = 256


def pack_kernel(ci_ref, og_ref, filter_ref, send_ref, taps_ref, sems):
    blocks, per, _ = ci_ref.shape
    k = lax.axis_index("ch")
    at = pl.multiple_of(8 * lax.div(k, 2), 8)
    copies = [
        pltpu.make_async_copy(filter_ref.at[pl.ds(at, 8), :], taps_ref, sems.at[0]),
        pltpu.make_async_copy(ci_ref, send_ref.at[:, 0:per, :], sems.at[1]),
        pltpu.make_async_copy(og_ref, send_ref.at[:, per : 2 * per, :], sems.at[2]),
    ]
    for copy in copies:
        copy.start()
    copies[0].wait()
    taps = taps_ref[...].astype(jnp.float32)
    taps = jnp.where(lax.rem(k, 2) == 0, taps[0:4, :], taps[4:8, :]).astype(jnp.bfloat16)
    for i in range(blocks):
        row = i * 4 // blocks
        send_ref[i, 2 * per : 2 * per + 1, :] = taps[row : row + 1, :]
    copies[1].wait()
    copies[2].wait()


def pack(conv_input, output_grad, long_filter, blocks):
    channels, own = conv_input.shape
    share = channels // blocks
    return pl.pallas_call(
        pack_kernel,
        out_shape=pltpu.VMEM((blocks, 2 * share + 1, own), jnp.bfloat16),
        in_specs=[pl.BlockSpec(memory_space=pl.ANY)] * 3,
        out_specs=pl.BlockSpec(memory_space=pltpu.VMEM),
        scratch_shapes=[pltpu.VMEM((8, own), jnp.bfloat16), pltpu.SemaphoreType.DMA((3,))],
        name="pack",
    )(
        conv_input.reshape(blocks, share, own),
        output_grad.reshape(blocks, share, own),
        long_filter,
    )


def roll_left(x, amount):
    lanes = x.shape[1]
    return x if amount == 0 else pltpu.roll(x, lanes - amount, 1)


def gradients_kernel(recv_ref, out_ref, og_ref, cit_ref, table_ref, skew_ref, acc_ref):
    blocks, _, own = recv_ref.shape
    per = 32
    tokens = blocks * own
    tiles = tokens // TILE
    rows = tiles * per

    ci = []
    for a in range(tiles):
        j, lo = (a * TILE) // own, (a * TILE) % own
        og_ref[a * per : (a + 1) * per, :] = recv_ref[j, per : 2 * per, lo : lo + TILE]
        ci.append(recv_ref[j, 0:per, lo : lo + TILE])
    og_ref[rows : 2 * rows, :] = jnp.zeros((rows, TILE), og_ref.dtype)
    cit_ref[...] = jnp.concatenate(ci, axis=0).T

    taps = jnp.concatenate(
        [recv_ref[j, 2 * per : 2 * per + 1, :].astype(jnp.float32) for j in range(blocks)], axis=1
    )
    wide = jnp.broadcast_to(taps, (8, tokens))
    base = pltpu.roll(wide, 0, 1, stride=1, stride_axis=0)
    for t in range(0, 16, 2):
        pair = jnp.concatenate(
            [base if t == 0 else pltpu.roll(base, 8 * t, 1), pltpu.roll(base, 8 * t + 8, 1)], axis=0
        )
        u = 8 * t + lax.broadcasted_iota(jnp.int32, (16, 128), 0)
        first = jnp.where(lax.broadcasted_iota(jnp.int32, (16, 128), 1) >= u, pair[:, 0:128], 0.0)
        pair = jnp.concatenate([first, pair[:, 128:]], axis=1).astype(jnp.bfloat16)
        table_ref[8 * t : 8 * t + 16, :] = pair
        table_ref[128 + 8 * t : 128 + 8 * t + 16, 128:] = pair[:, : tokens - 128]
        table_ref[128 + 8 * t : 128 + 8 * t + 16, 0:128] = jnp.zeros((16, 128), jnp.bfloat16)

    for d in range(tiles):
        depth = rows if d < tiles // 2 else rows // 2
        cross = jnp.dot(
            cit_ref[:, 0:depth],
            og_ref[d * per : d * per + depth, :],
            preferred_element_type=jnp.float32,
        )
        if d == 0:
            u = lax.broadcasted_iota(jnp.int32, (TILE, TILE), 0)
            v = lax.broadcasted_iota(jnp.int32, (TILE, TILE), 1)
            cross = jnp.where(v >= u, cross, 0.0)
        upper, lower = cross[0:128, :], cross[128:256, :]
        at = d * TILE
        skew_ref[:, at : at + 128] = upper[:, 0:128] + lower[:, 128:256]
        skew_ref[:, at + 128 : at + 256] = upper[:, 128:256]
        if d > 0:
            skew_ref[:, at - 128 : at] = skew_ref[:, at - 128 : at] + lower[:, 0:128]
    folded = skew_ref[0:8, :]
    for t in range(1, 16):
        folded = folded + roll_left(skew_ref[8 * t : 8 * t + 8, :], 8 * t)
    r = lax.broadcasted_iota(jnp.int32, folded.shape, 0)
    for bit in (1, 2, 4):
        folded = jnp.where((r & bit) > 0, roll_left(folded, bit), folded)
    lags = jnp.sum(folded, axis=0, keepdims=True)
    high = lags.astype(jnp.bfloat16).astype(jnp.float32)
    low = lags - high
    row = lax.broadcasted_iota(jnp.int32, (8, own), 0)
    for j in range(blocks):
        part = slice(j * own, (j + 1) * own)
        packed = jnp.where(row == 0, high[:, part], jnp.where(row == 1, low[:, part], 0.0))
        out_ref[j, per : per + 8, :] = packed.astype(jnp.bfloat16)

    for d in range(tiles):
        live = rows - d * per
        term = lax.dot_general(
            og_ref[d * per : rows, :],
            table_ref[:, d * TILE : (d + 1) * TILE],
            (((1,), (1,)), ((), ())),
            preferred_element_type=jnp.float32,
        )
        if d == 0:
            acc_ref[...] = term
        else:
            acc_ref[0:live, :] = acc_ref[0:live, :] + term
    for a in range(tiles):
        j, lo = (a * TILE) // own, (a * TILE) % own
        out_ref[j, 0:per, lo : lo + TILE] = acc_ref[a * per : (a + 1) * per, :].astype(jnp.bfloat16)


def gradients(recv):
    blocks, _, own = recv.shape
    tokens = blocks * own
    rows = tokens // TILE * 32
    return pl.pallas_call(
        gradients_kernel,
        out_shape=pltpu.VMEM((blocks, 40, own), jnp.bfloat16),
        in_specs=[pl.BlockSpec(memory_space=pltpu.VMEM)],
        out_specs=pl.BlockSpec(memory_space=pltpu.VMEM),
        scratch_shapes=[
            pltpu.VMEM((2 * rows, TILE), jnp.bfloat16),
            pltpu.VMEM((TILE, rows), jnp.bfloat16),
            pltpu.VMEM((TILE, tokens), jnp.bfloat16),
            pltpu.VMEM((128, tokens), jnp.float32),
            pltpu.VMEM((rows, TILE), jnp.float32),
        ],
        name="gradients",
    )(pltpu.with_memory_space_constraint(recv, pltpu.VMEM))


def per_device(conv_input, output_grad, long_filter):
    channels, own = conv_input.shape
    cycle = lax.axis_size("ctx")
    share = channels // cycle
    groups_here = channels // (C // G)
    send = pack(conv_input, output_grad, long_filter, cycle)
    recv = lax.all_to_all(send, "ctx", 0, 0, tiled=True)
    back = lax.all_to_all(gradients(recv), "ctx", 0, 0, tiled=True)
    input_grad = back[:, :share, :].reshape(channels, own)
    parts = back[:, share : share + 2, :].astype(jnp.float32)
    owned = jnp.sum(parts.reshape(groups_here, -1, own), axis=1)
    peers = lax.axis_size("ch")
    groups = [list(range(core, peers, 2)) for core in range(2)]
    mine = lax.all_to_all(
        jnp.broadcast_to(owned[None], (peers // 2, groups_here, own)),
        "ch",
        0,
        0,
        axis_index_groups=groups,
        tiled=True,
    )
    theirs = lax.ppermute(mine, "ch", [(k, k ^ 1) for k in range(peers)])
    filter_grad = jnp.where(
        lax.axis_index("ch") % 2 == 0,
        jnp.concatenate([mine, theirs], axis=1),
        jnp.concatenate([theirs, mine], axis=1),
    )
    return input_grad, filter_grad.reshape(G, own)


def solution(mesh):
    in_specs = (P("ch", "ctx"), P("ch", "ctx"), P(None, "ctx"))
    out_specs = (P("ch", "ctx"), P(None, "ctx"))
    return jax.shard_map(
        per_device, mesh=mesh, in_specs=in_specs, out_specs=out_specs, check_vma=False
    )
```

```python
import jax
import jax.numpy as jnp
from jax import lax
from jax.experimental import pallas as pl
from jax.experimental.pallas import tpu as pltpu
from jax.sharding import PartitionSpec as P

C = 8192
G = 128
TILE = 256


def pack_kernel(ci_ref, og_ref, filter_ref, send_ref, taps_ref, sems):
    blocks, per, own = ci_ref.shape
    pieces = own // 128
    span = pieces * per
    k = lax.axis_index("ch")
    at = pl.multiple_of(8 * lax.div(k, 2), 8)
    taps_copy = pltpu.make_async_copy(filter_ref.at[pl.ds(at, 8), :], taps_ref, sems.at[0])
    taps_copy.start()
    copies = []
    for n, ref in enumerate((ci_ref, og_ref)):
        for q in range(pieces):
            copy = pltpu.make_async_copy(
                ref.at[:, :, q * 128 : (q + 1) * 128],
                send_ref.at[:, n * span + q * per : n * span + (q + 1) * per, :],
                sems.at[1 + n * pieces + q],
            )
            copy.start()
            copies.append(copy)
    taps_copy.wait()
    taps = taps_ref[...].astype(jnp.float32)
    taps = jnp.where(lax.rem(k, 2) == 0, taps[0:4, :], taps[4:8, :])
    for g in range(4):
        rows = [taps[g : g + 1, q * 128 : (q + 1) * 128] for q in range(pieces)]
        block = jnp.concatenate(rows + rows, axis=0).astype(jnp.bfloat16)
        for i in range(g * blocks // 4, (g + 1) * blocks // 4):
            send_ref[i, 2 * span : 2 * span + 8, :] = block
    for copy in copies:
        copy.wait()


def pack(conv_input, output_grad, long_filter, blocks):
    channels, own = conv_input.shape
    share = channels // blocks
    pieces = own // 128
    return pl.pallas_call(
        pack_kernel,
        out_shape=pltpu.VMEM((blocks, 2 * pieces * share + 8, 128), jnp.bfloat16),
        in_specs=[pl.BlockSpec(memory_space=pl.ANY)] * 3,
        out_specs=pl.BlockSpec(memory_space=pltpu.VMEM),
        scratch_shapes=[
            pltpu.VMEM((8, own), jnp.bfloat16),
            pltpu.SemaphoreType.DMA((1 + 2 * pieces,)),
        ],
        name="pack",
    )(
        conv_input.reshape(blocks, share, own),
        output_grad.reshape(blocks, share, own),
        long_filter,
    )


def roll_left(x, amount):
    lanes = x.shape[1]
    return x if amount == 0 else pltpu.roll(x, lanes - amount, 1)


def gradients_kernel(recv_ref, out_ref, og_ref, cit_ref, table_ref, skew_ref, acc_ref):
    blocks, height, _ = recv_ref.shape
    per = 32
    pieces = (height - 8) // (2 * per)
    span = pieces * per
    own = pieces * 128
    tokens = blocks * own
    tiles = tokens // TILE
    rows = tiles * per

    ci = []
    for a in range(tiles):
        j, q = divmod(2 * a, pieces)
        left, right = slice(q * per, (q + 1) * per), slice((q + 1) * per, (q + 2) * per)
        og_ref[a * per : (a + 1) * per, 0:128] = recv_ref[j, span + left.start : span + left.stop, :]
        og_ref[a * per : (a + 1) * per, 128:256] = recv_ref[
            j, span + right.start : span + right.stop, :
        ]
        ci.append(jnp.concatenate([recv_ref[j, left, :], recv_ref[j, right, :]], axis=1))
    og_ref[rows : 2 * rows, :] = jnp.zeros((rows, TILE), og_ref.dtype)
    cit_ref[...] = jnp.concatenate(ci, axis=0).T

    taps = [recv_ref[j, 2 * span : 2 * span + 8, :].astype(jnp.float32) for j in range(blocks)]
    taps = jnp.concatenate([x[q : q + 1, :] for x in taps for q in range(pieces)], axis=1)
    wide = jnp.broadcast_to(taps, (8, tokens))
    base = pltpu.roll(wide, 0, 1, stride=1, stride_axis=0)
    for t in range(0, 16, 2):
        pair = jnp.concatenate(
            [base if t == 0 else pltpu.roll(base, 8 * t, 1), pltpu.roll(base, 8 * t + 8, 1)], axis=0
        )
        u = 8 * t + lax.broadcasted_iota(jnp.int32, (16, 128), 0)
        first = jnp.where(lax.broadcasted_iota(jnp.int32, (16, 128), 1) >= u, pair[:, 0:128], 0.0)
        pair = jnp.concatenate([first, pair[:, 128:]], axis=1).astype(jnp.bfloat16)
        table_ref[8 * t : 8 * t + 16, :] = pair
        table_ref[128 + 8 * t : 128 + 8 * t + 16, 128:] = pair[:, : tokens - 128]
        table_ref[128 + 8 * t : 128 + 8 * t + 16, 0:128] = jnp.zeros((16, 128), jnp.bfloat16)

    for d in range(tiles):
        depth = rows if d < tiles // 2 else rows // 2
        cross = jnp.dot(
            cit_ref[:, 0:depth],
            og_ref[d * per : d * per + depth, :],
            preferred_element_type=jnp.float32,
        )
        if d == 0:
            u = lax.broadcasted_iota(jnp.int32, (TILE, TILE), 0)
            v = lax.broadcasted_iota(jnp.int32, (TILE, TILE), 1)
            cross = jnp.where(v >= u, cross, 0.0)
        upper, lower = cross[0:128, :], cross[128:256, :]
        at = d * TILE
        skew_ref[:, at : at + 128] = upper[:, 0:128] + lower[:, 128:256]
        skew_ref[:, at + 128 : at + 256] = upper[:, 128:256]
        if d > 0:
            skew_ref[:, at - 128 : at] = skew_ref[:, at - 128 : at] + lower[:, 0:128]
    folded = skew_ref[0:8, :]
    for t in range(1, 16):
        folded = folded + roll_left(skew_ref[8 * t : 8 * t + 8, :], 8 * t)
    r = lax.broadcasted_iota(jnp.int32, folded.shape, 0)
    for bit in (1, 2, 4):
        folded = jnp.where((r & bit) > 0, roll_left(folded, bit), folded)
    lags = jnp.sum(folded, axis=0, keepdims=True)
    high = lags.astype(jnp.bfloat16).astype(jnp.float32)
    low = lags - high
    for j in range(blocks):
        packed = [
            part[:, at : at + 128]
            for part in (high, low)
            for at in range(j * own, (j + 1) * own, 128)
        ]
        out_ref[j, span : span + 8, :] = jnp.concatenate(packed, axis=0).astype(jnp.bfloat16)

    for d in range(tiles):
        live = rows - d * per
        term = lax.dot_general(
            og_ref[d * per : rows, :],
            table_ref[:, d * TILE : (d + 1) * TILE],
            (((1,), (1,)), ((), ())),
            preferred_element_type=jnp.float32,
        )
        if d == 0:
            acc_ref[...] = term
        else:
            acc_ref[0:live, :] = acc_ref[0:live, :] + term
    for a in range(tiles):
        j, q = divmod(2 * a, pieces)
        done = acc_ref[a * per : (a + 1) * per, :].astype(jnp.bfloat16)
        out_ref[j, q * per : (q + 1) * per, :] = done[:, 0:128]
        out_ref[j, (q + 1) * per : (q + 2) * per, :] = done[:, 128:256]


def gradients(recv):
    blocks, height, _ = recv.shape
    span = (height - 8) // 2
    tokens = blocks * span * 128 // 32
    rows = tokens // TILE * 32
    return pl.pallas_call(
        gradients_kernel,
        out_shape=pltpu.VMEM((blocks, span + 8, 128), jnp.bfloat16),
        in_specs=[pl.BlockSpec(memory_space=pltpu.VMEM)],
        out_specs=pl.BlockSpec(memory_space=pltpu.VMEM),
        scratch_shapes=[
            pltpu.VMEM((2 * rows, TILE), jnp.bfloat16),
            pltpu.VMEM((TILE, rows), jnp.bfloat16),
            pltpu.VMEM((TILE, tokens), jnp.bfloat16),
            pltpu.VMEM((128, tokens), jnp.float32),
            pltpu.VMEM((rows, TILE), jnp.float32),
        ],
        name="gradients",
    )(pltpu.with_memory_space_constraint(recv, pltpu.VMEM))


def spread_kernel(back_ref, out_ref):
    blocks, height, _ = back_ref.shape
    receivers, groups, own = out_ref.shape
    pieces = own // 128
    parts = [back_ref[i, height - 8 : height, :].astype(jnp.float32) for i in range(blocks)]
    parts = [x[0:pieces, :] + x[pieces : 2 * pieces, :] for x in parts]
    each = blocks // groups
    sums = [sum(parts[g * each + 1 : (g + 1) * each], parts[g * each]) for g in range(groups)]
    owned = jnp.concatenate(
        [jnp.concatenate([x[q : q + 1, :] for x in sums], axis=0) for q in range(pieces)], axis=1
    )
    for n in range(receivers):
        out_ref[n, :, :] = owned


def spread(back, receivers, groups, own):
    return pl.pallas_call(
        spread_kernel,
        out_shape=pltpu.VMEM((receivers, groups, own), jnp.float32),
        in_specs=[pl.BlockSpec(memory_space=pltpu.VMEM)],
        out_specs=pl.BlockSpec(memory_space=pltpu.VMEM),
        name="spread",
    )(back)


def finish_kernel(back_ref, mine_ref, theirs_ref, ig_ref, fg_ref, both_ref, sems):
    blocks, share, own = ig_ref.shape
    senders, groups, _ = mine_ref.shape
    copies = []
    for q in range(own // 128):
        copies.append(
            pltpu.make_async_copy(
                back_ref.at[:, q * share : (q + 1) * share, :],
                ig_ref.at[:, :, q * 128 : (q + 1) * 128],
                sems.at[q],
            )
        )
    for copy in copies:
        copy.start()
    first = lax.rem(lax.axis_index("ch"), 2) == 0
    half = senders // 2
    for part in range(2):
        for n in range(part * half, (part + 1) * half):
            mine, theirs = mine_ref[n, :, :], theirs_ref[n, :, :]
            both_ref[n, 0:groups, :] = jnp.where(first, mine, theirs)
            both_ref[n, groups : 2 * groups, :] = jnp.where(first, theirs, mine)
        copy = pltpu.make_async_copy(
            both_ref.at[part * half : (part + 1) * half],
            fg_ref.at[part * half : (part + 1) * half],
            sems.at[own // 128 + part],
        )
        copy.start()
        copies.append(copy)
    for copy in copies:
        copy.wait()


def finish(back, mine, theirs, share, own):
    senders, groups, _ = mine.shape
    return pl.pallas_call(
        finish_kernel,
        out_shape=(
            jax.ShapeDtypeStruct((back.shape[0], share, own), jnp.bfloat16),
            jax.ShapeDtypeStruct((senders, 2 * groups, own), jnp.float32),
        ),
        in_specs=[pl.BlockSpec(memory_space=pltpu.VMEM)] * 3,
        out_specs=(pl.BlockSpec(memory_space=pl.ANY),) * 2,
        scratch_shapes=[
            pltpu.VMEM((senders, 2 * groups, own), jnp.float32),
            pltpu.SemaphoreType.DMA((own // 128 + 2,)),
        ],
        name="finish",
    )(*(pltpu.with_memory_space_constraint(x, pltpu.VMEM) for x in (back, mine, theirs)))


def per_device(conv_input, output_grad, long_filter):
    channels, own = conv_input.shape
    cycle = lax.axis_size("ctx")
    share = channels // cycle
    groups_here = channels // (C // G)
    send = pack(conv_input, output_grad, long_filter, cycle)
    recv = lax.all_to_all(send, "ctx", 0, 0, tiled=True)
    back = lax.all_to_all(gradients(recv), "ctx", 0, 0, tiled=True)
    back = pltpu.with_memory_space_constraint(back, pltpu.VMEM)
    peers = lax.axis_size("ch")
    mine = lax.all_to_all(
        spread(back, peers // 2, groups_here, own),
        "ch",
        0,
        0,
        axis_index_groups=[list(range(core, peers, 2)) for core in range(2)],
        tiled=True,
    )
    theirs = lax.ppermute(mine, "ch", [(k, k ^ 1) for k in range(peers)])
    input_grad, filter_grad = finish(back, mine, theirs, share, own)
    return input_grad.reshape(channels, own), filter_grad.reshape(G, own)


def solution(mesh):
    in_specs = (P("ch", "ctx"), P("ch", "ctx"), P(None, "ctx"))
    out_specs = (P("ch", "ctx"), P(None, "ctx"))
    return jax.shard_map(
        per_device, mesh=mesh, in_specs=in_specs, out_specs=out_specs, check_vma=False
    )
```

```python
import jax
import jax.numpy as jnp
from jax import lax
from jax.experimental import pallas as pl
from jax.experimental.pallas import tpu as pltpu
from jax.sharding import PartitionSpec as P

C = 8192
G = 128
TILE = 256
FIRST_CTX = 6
FIRST_CHIP = 4


def pack_kernel(ci_ref, og_ref, filter_ref, send_ref, taps_ref, sems):
    blocks, per, own = ci_ref.shape
    pieces = own // 128
    span = pieces * per
    k = lax.axis_index("ch")
    at = pl.multiple_of(8 * lax.div(k, 2), 8)
    taps_copy = pltpu.make_async_copy(filter_ref.at[pl.ds(at, 8), :], taps_ref, sems.at[0])
    taps_copy.start()
    copies = []
    for n, ref in enumerate((ci_ref, og_ref)):
        for q in range(pieces):
            copy = pltpu.make_async_copy(
                ref.at[:, :, q * 128 : (q + 1) * 128],
                send_ref.at[:, n * span + q * per : n * span + (q + 1) * per, :],
                sems.at[1 + n * pieces + q],
            )
            copy.start()
            copies.append(copy)
    taps_copy.wait()
    taps = taps_ref[...].astype(jnp.float32)
    taps = jnp.where(lax.rem(k, 2) == 0, taps[0:4, :], taps[4:8, :])
    for g in range(4):
        rows = [taps[g : g + 1, q * 128 : (q + 1) * 128] for q in range(pieces)]
        block = jnp.concatenate(rows + rows, axis=0).astype(jnp.bfloat16)
        for i in range(g * blocks // 4, (g + 1) * blocks // 4):
            send_ref[i, 2 * span : 2 * span + 8, :] = block
    for copy in copies:
        copy.wait()


def pack(conv_input, output_grad, long_filter, blocks):
    channels, own = conv_input.shape
    share = channels // blocks
    pieces = own // 128
    return pl.pallas_call(
        pack_kernel,
        out_shape=pltpu.VMEM((blocks, 2 * pieces * share + 8, 128), jnp.bfloat16),
        in_specs=[pl.BlockSpec(memory_space=pl.ANY)] * 3,
        out_specs=pl.BlockSpec(memory_space=pltpu.VMEM),
        scratch_shapes=[
            pltpu.VMEM((8, own), jnp.bfloat16),
            pltpu.SemaphoreType.DMA((1 + 2 * pieces,)),
        ],
        name="pack",
    )(
        conv_input.reshape(blocks, share, own),
        output_grad.reshape(blocks, share, own),
        long_filter,
    )


def roll_left(x, amount):
    lanes = x.shape[1]
    return x if amount == 0 else pltpu.roll(x, lanes - amount, 1)


def gradients_kernel(recv_ref, out_ref, og_ref, cit_ref, table_ref, skew_ref, acc_ref):
    blocks, height, _ = recv_ref.shape
    per = 32
    pieces = (height - 8) // (2 * per)
    span = pieces * per
    own = pieces * 128
    tokens = blocks * own
    tiles = tokens // TILE
    rows = tiles * per

    ci = []
    for a in range(tiles):
        j, q = divmod(2 * a, pieces)
        j = j ^ FIRST_CTX
        left, right = slice(q * per, (q + 1) * per), slice((q + 1) * per, (q + 2) * per)
        og_ref[a * per : (a + 1) * per, 0:128] = recv_ref[j, span + left.start : span + left.stop, :]
        og_ref[a * per : (a + 1) * per, 128:256] = recv_ref[
            j, span + right.start : span + right.stop, :
        ]
        ci.append(jnp.concatenate([recv_ref[j, left, :], recv_ref[j, right, :]], axis=1))
    og_ref[rows : 2 * rows, :] = jnp.zeros((rows, TILE), og_ref.dtype)
    cit_ref[...] = jnp.concatenate(ci, axis=0).T

    taps = [
        recv_ref[j ^ FIRST_CTX, 2 * span : 2 * span + 8, :].astype(jnp.float32)
        for j in range(blocks)
    ]
    taps = jnp.concatenate([x[q : q + 1, :] for x in taps for q in range(pieces)], axis=1)
    wide = jnp.broadcast_to(taps, (8, tokens))
    base = pltpu.roll(wide, 0, 1, stride=1, stride_axis=0)
    for t in range(0, 16, 2):
        pair = jnp.concatenate(
            [base if t == 0 else pltpu.roll(base, 8 * t, 1), pltpu.roll(base, 8 * t + 8, 1)], axis=0
        )
        u = 8 * t + lax.broadcasted_iota(jnp.int32, (16, 128), 0)
        first = jnp.where(lax.broadcasted_iota(jnp.int32, (16, 128), 1) >= u, pair[:, 0:128], 0.0)
        pair = jnp.concatenate([first, pair[:, 128:]], axis=1).astype(jnp.bfloat16)
        table_ref[8 * t : 8 * t + 16, :] = pair
        table_ref[128 + 8 * t : 128 + 8 * t + 16, 128:] = pair[:, : tokens - 128]
        table_ref[128 + 8 * t : 128 + 8 * t + 16, 0:128] = jnp.zeros((16, 128), jnp.bfloat16)

    for d in range(tiles):
        depth = rows if d < tiles // 2 else rows // 2
        cross = jnp.dot(
            cit_ref[:, 0:depth],
            og_ref[d * per : d * per + depth, :],
            preferred_element_type=jnp.float32,
        )
        if d == 0:
            u = lax.broadcasted_iota(jnp.int32, (TILE, TILE), 0)
            v = lax.broadcasted_iota(jnp.int32, (TILE, TILE), 1)
            cross = jnp.where(v >= u, cross, 0.0)
        upper, lower = cross[0:128, :], cross[128:256, :]
        at = d * TILE
        skew_ref[:, at : at + 128] = upper[:, 0:128] + lower[:, 128:256]
        skew_ref[:, at + 128 : at + 256] = upper[:, 128:256]
        if d > 0:
            skew_ref[:, at - 128 : at] = skew_ref[:, at - 128 : at] + lower[:, 0:128]
    folded = skew_ref[0:8, :]
    for t in range(1, 16):
        folded = folded + roll_left(skew_ref[8 * t : 8 * t + 8, :], 8 * t)
    r = lax.broadcasted_iota(jnp.int32, folded.shape, 0)
    for bit in (1, 2, 4):
        folded = jnp.where((r & bit) > 0, roll_left(folded, bit), folded)
    lags = jnp.sum(folded, axis=0, keepdims=True)
    high = lags.astype(jnp.bfloat16).astype(jnp.float32)
    low = lags - high
    for j in range(blocks):
        packed = [
            part[:, at : at + 128]
            for part in (high, low)
            for at in range(j * own, (j + 1) * own, 128)
        ]
        out_ref[j ^ FIRST_CTX, span : span + 8, :] = jnp.concatenate(packed, axis=0).astype(jnp.bfloat16)

    for d in range(tiles):
        live = rows - d * per
        term = lax.dot_general(
            og_ref[d * per : rows, :],
            table_ref[:, d * TILE : (d + 1) * TILE],
            (((1,), (1,)), ((), ())),
            preferred_element_type=jnp.float32,
        )
        if d == 0:
            acc_ref[...] = term
        else:
            acc_ref[0:live, :] = acc_ref[0:live, :] + term
    for a in range(tiles):
        j, q = divmod(2 * a, pieces)
        j = j ^ FIRST_CTX
        done = acc_ref[a * per : (a + 1) * per, :].astype(jnp.bfloat16)
        out_ref[j, q * per : (q + 1) * per, :] = done[:, 0:128]
        out_ref[j, (q + 1) * per : (q + 2) * per, :] = done[:, 128:256]


def gradients(recv):
    blocks, height, _ = recv.shape
    span = (height - 8) // 2
    tokens = blocks * span * 128 // 32
    rows = tokens // TILE * 32
    return pl.pallas_call(
        gradients_kernel,
        out_shape=pltpu.VMEM((blocks, span + 8, 128), jnp.bfloat16),
        in_specs=[pl.BlockSpec(memory_space=pltpu.VMEM)],
        out_specs=pl.BlockSpec(memory_space=pltpu.VMEM),
        scratch_shapes=[
            pltpu.VMEM((2 * rows, TILE), jnp.bfloat16),
            pltpu.VMEM((TILE, rows), jnp.bfloat16),
            pltpu.VMEM((TILE, tokens), jnp.bfloat16),
            pltpu.VMEM((128, tokens), jnp.float32),
            pltpu.VMEM((rows, TILE), jnp.float32),
        ],
        name="gradients",
    )(pltpu.with_memory_space_constraint(recv, pltpu.VMEM))


def spread_kernel(back_ref, out_ref):
    blocks, height, _ = back_ref.shape
    receivers, groups, own = out_ref.shape
    pieces = own // 128
    parts = [back_ref[i, height - 8 : height, :].astype(jnp.float32) for i in range(blocks)]
    parts = [x[0:pieces, :] + x[pieces : 2 * pieces, :] for x in parts]
    each = blocks // groups
    sums = [sum(parts[g * each + 1 : (g + 1) * each], parts[g * each]) for g in range(groups)]
    owned = jnp.concatenate(
        [jnp.concatenate([x[q : q + 1, :] for x in sums], axis=0) for q in range(pieces)], axis=1
    )
    for n in range(receivers):
        out_ref[n, :, :] = owned


def spread(back, receivers, groups, own):
    return pl.pallas_call(
        spread_kernel,
        out_shape=pltpu.VMEM((receivers, groups, own), jnp.float32),
        in_specs=[pl.BlockSpec(memory_space=pltpu.VMEM)],
        out_specs=pl.BlockSpec(memory_space=pltpu.VMEM),
        name="spread",
    )(back)


def finish_kernel(back_ref, mine_ref, theirs_ref, ig_ref, fg_ref, both_ref, sems):
    blocks, share, own = ig_ref.shape
    senders, groups, _ = mine_ref.shape
    copies = []
    for q in range(own // 128):
        copies.append(
            pltpu.make_async_copy(
                back_ref.at[:, q * share : (q + 1) * share, :],
                ig_ref.at[:, :, q * 128 : (q + 1) * 128],
                sems.at[q],
            )
        )
    for copy in copies:
        copy.start()
    first = lax.rem(lax.axis_index("ch"), 2) == 0
    half = senders // 2
    for part in range(2):
        for n in range(part * half, (part + 1) * half):
            mine, theirs = mine_ref[n ^ FIRST_CHIP, :, :], theirs_ref[n ^ FIRST_CHIP, :, :]
            both_ref[n, 0:groups, :] = jnp.where(first, mine, theirs)
            both_ref[n, groups : 2 * groups, :] = jnp.where(first, theirs, mine)
        copy = pltpu.make_async_copy(
            both_ref.at[part * half : (part + 1) * half],
            fg_ref.at[part * half : (part + 1) * half],
            sems.at[own // 128 + part],
        )
        copy.start()
        copies.append(copy)
    for copy in copies:
        copy.wait()


def finish(back, mine, theirs, share, own):
    senders, groups, _ = mine.shape
    return pl.pallas_call(
        finish_kernel,
        out_shape=(
            jax.ShapeDtypeStruct((back.shape[0], share, own), jnp.bfloat16),
            jax.ShapeDtypeStruct((senders, 2 * groups, own), jnp.float32),
        ),
        in_specs=[pl.BlockSpec(memory_space=pltpu.VMEM)] * 3,
        out_specs=(pl.BlockSpec(memory_space=pl.ANY),) * 2,
        scratch_shapes=[
            pltpu.VMEM((senders, 2 * groups, own), jnp.float32),
            pltpu.SemaphoreType.DMA((own // 128 + 2,)),
        ],
        name="finish",
    )(*(pltpu.with_memory_space_constraint(x, pltpu.VMEM) for x in (back, mine, theirs)))


def per_device(conv_input, output_grad, long_filter):
    channels, own = conv_input.shape
    cycle = lax.axis_size("ctx")
    share = channels // cycle
    groups_here = channels // (C // G)
    send = pack(conv_input, output_grad, long_filter, cycle)
    ring = [[p ^ FIRST_CTX for p in range(cycle)]]
    recv = lax.all_to_all(send, "ctx", 0, 0, axis_index_groups=ring, tiled=True)
    back = lax.all_to_all(gradients(recv), "ctx", 0, 0, axis_index_groups=ring, tiled=True)
    back = pltpu.with_memory_space_constraint(back, pltpu.VMEM)
    peers = lax.axis_size("ch")
    mine = lax.all_to_all(
        spread(back, peers // 2, groups_here, own),
        "ch",
        0,
        0,
        axis_index_groups=[
            [2 * (p ^ FIRST_CHIP) + core for p in range(peers // 2)] for core in range(2)
        ],
        tiled=True,
    )
    theirs = lax.ppermute(mine, "ch", [(k, k ^ 1) for k in range(peers)])
    input_grad, filter_grad = finish(back, mine, theirs, share, own)
    return input_grad.reshape(channels, own), filter_grad.reshape(G, own)


def solution(mesh):
    in_specs = (P("ch", "ctx"), P("ch", "ctx"), P(None, "ctx"))
    out_specs = (P("ch", "ctx"), P(None, "ctx"))
    return jax.shard_map(
        per_device, mesh=mesh, in_specs=in_specs, out_specs=out_specs, check_vma=False
    )
```

```python
import jax
import jax.numpy as jnp
from jax import lax
from jax.experimental import pallas as pl
from jax.experimental.pallas import tpu as pltpu
from jax.sharding import PartitionSpec as P

C = 8192
G = 128
TILE = 256
FIRST_CTX = 6
FIRST_CHIP = 4
CTX_SLOT = [j ^ FIRST_CTX for j in range(8)]


def pack_kernel(ci_ref, og_ref, filter_ref, send_ref, taps_ref, sems):
    blocks, span, _ = ci_ref.shape
    pieces = filter_ref.shape[1] // 128
    k = lax.axis_index("ch")
    at = pl.multiple_of(8 * lax.div(k, 2), 8)
    copies = [
        pltpu.make_async_copy(filter_ref.at[pl.ds(at, 8), :], taps_ref, sems.at[0]),
        pltpu.make_async_copy(ci_ref, send_ref.at[:, 0:span, :], sems.at[1]),
        pltpu.make_async_copy(og_ref, send_ref.at[:, span : 2 * span, :], sems.at[2]),
    ]
    for copy in copies:
        copy.start()
    copies[0].wait()
    taps = taps_ref[...].astype(jnp.float32)
    taps = jnp.where(lax.rem(k, 2) == 0, taps[0:4, :], taps[4:8, :])
    for g in range(4):
        rows = [taps[g : g + 1, q * 128 : (q + 1) * 128] for q in range(pieces)]
        block = jnp.concatenate(rows + rows, axis=0).astype(jnp.bfloat16)
        for i in range(g * blocks // 4, (g + 1) * blocks // 4):
            send_ref[i, 2 * span : 2 * span + 8, :] = block
    copies[1].wait()
    copies[2].wait()


def tiles_of(x, blocks):
    channels, own = x.shape
    x = x.reshape(channels // 8, 8, own // 128, 128).transpose(0, 2, 1, 3)
    return x.reshape(blocks, channels * own // (128 * blocks), 128)


def pack(conv_input, output_grad, long_filter, blocks):
    channels, own = conv_input.shape
    span = channels * own // (128 * blocks)
    return pl.pallas_call(
        pack_kernel,
        out_shape=pltpu.VMEM((blocks, 2 * span + 8, 128), jnp.bfloat16),
        in_specs=[pl.BlockSpec(memory_space=pl.ANY)] * 3,
        out_specs=pl.BlockSpec(memory_space=pltpu.VMEM),
        scratch_shapes=[pltpu.VMEM((8, own), jnp.bfloat16), pltpu.SemaphoreType.DMA((3,))],
        name="pack",
    )(tiles_of(conv_input, blocks), tiles_of(output_grad, blocks), long_filter)


def roll_left(x, amount):
    lanes = x.shape[1]
    return x if amount == 0 else pltpu.roll(x, lanes - amount, 1)


def gradients_kernel(
    recv_ref, out_ref, og_ref, pair_ref, cit_ref, table_ref, skew_ref, acc_ref
):
    blocks, height, _ = recv_ref.shape
    per = 32
    pieces = (height - 8) // (2 * per)
    span = pieces * per
    own = pieces * 128
    tokens = blocks * own
    tiles = tokens // TILE
    rows = tiles * per
    small = tokens // 128

    def piece(base, a, r):
        j, q = divmod(a, pieces)
        at = base + (r * pieces + q) * 8
        return recv_ref[CTX_SLOT[j], at : at + 8, :]

    for a in range(small):
        for r in range(per // 8):
            x = piece(span, a, r)
            to = slice(a * per + r * 8, a * per + r * 8 + 8)
            pair_ref[to, 0:128] = x
            if a > 0:
                pair_ref[to.start - per : to.stop - per, 128:256] = x
            to = slice(a // 2 * per + r * 8, a // 2 * per + r * 8 + 8)
            og_ref[to, (a % 2) * 128 : (a % 2) * 128 + 128] = x
    pair_ref[(small - 1) * per : small * per, 128:256] = jnp.zeros((per, 128), pair_ref.dtype)
    pair_ref[small * per :, :] = jnp.zeros((pair_ref.shape[0] - small * per, TILE), pair_ref.dtype)
    for m in range(small // 8):
        ci = [piece(0, a, r) for a in range(8 * m, 8 * m + 8) for r in range(per // 8)]
        cit_ref[m * 128 : (m + 1) * 128, :] = jnp.concatenate(ci, axis=0).T

    taps = [
        recv_ref[CTX_SLOT[j], 2 * span : 2 * span + 8, :].astype(jnp.float32)
        for j in range(blocks)
    ]
    taps = jnp.concatenate([x[q : q + 1, :] for x in taps for q in range(pieces)], axis=1)
    wide = jnp.broadcast_to(taps, (8, tokens))
    base = pltpu.roll(wide, 0, 1, stride=1, stride_axis=0)
    for t in range(0, 16, 2):
        pair = jnp.concatenate(
            [base if t == 0 else pltpu.roll(base, 8 * t, 1), pltpu.roll(base, 8 * t + 8, 1)], axis=0
        )
        u = 8 * t + lax.broadcasted_iota(jnp.int32, (16, 128), 0)
        first = jnp.where(lax.broadcasted_iota(jnp.int32, (16, 128), 1) >= u, pair[:, 0:128], 0.0)
        pair = jnp.concatenate([first, pair[:, 128:]], axis=1).astype(jnp.bfloat16)
        table_ref[8 * t : 8 * t + 16, :] = pair
        table_ref[128 + 8 * t : 128 + 8 * t + 16, 128:] = pair[:, : tokens - 128]
        table_ref[128 + 8 * t : 128 + 8 * t + 16, 0:128] = jnp.zeros((16, 128), jnp.bfloat16)

    for n in range(tiles):
        parts = n // 4 + 1
        cross = jnp.dot(
            cit_ref[0 : parts * 128, :],
            pair_ref[n * 2 * per : n * 2 * per + 8 * per, :],
            preferred_element_type=jnp.float32,
        )
        for m in range(parts):
            term = cross[m * 128 : (m + 1) * 128, :]
            d = n - 4 * m
            if d == 0:
                u = lax.broadcasted_iota(jnp.int32, (128, TILE), 0)
                v = lax.broadcasted_iota(jnp.int32, (128, TILE), 1)
                term = jnp.where(v >= u, term, 0.0)
            to = slice(d * TILE, (d + 1) * TILE)
            skew_ref[:, to] = term if m == 0 else skew_ref[:, to] + term
    folded = skew_ref[0:8, :]
    for t in range(1, 16):
        folded = folded + roll_left(skew_ref[8 * t : 8 * t + 8, :], 8 * t)
    r = lax.broadcasted_iota(jnp.int32, folded.shape, 0)
    for bit in (1, 2, 4):
        folded = jnp.where((r & bit) > 0, roll_left(folded, bit), folded)
    lags = jnp.sum(folded, axis=0, keepdims=True)
    high = lags.astype(jnp.bfloat16).astype(jnp.float32)
    low = lags - high
    for j in range(blocks):
        packed = [
            part[:, at : at + 128]
            for part in (high, low)
            for at in range(j * own, (j + 1) * own, 128)
        ]
        out_ref[CTX_SLOT[j], span : span + 8, :] = jnp.concatenate(packed, axis=0).astype(jnp.bfloat16)

    for d in range(tiles):
        live = rows - d * per
        term = lax.dot_general(
            og_ref[d * per : rows, :],
            table_ref[:, d * TILE : (d + 1) * TILE],
            (((1,), (1,)), ((), ())),
            preferred_element_type=jnp.float32,
        )
        if d == 0:
            acc_ref[...] = term
        else:
            acc_ref[0:live, :] = acc_ref[0:live, :] + term
    for a in range(tiles):
        j, q = divmod(2 * a, pieces)
        done = acc_ref[a * per : (a + 1) * per, :].astype(jnp.bfloat16)
        for r in range(per // 8):
            at = (r * pieces + q) * 8
            out_ref[CTX_SLOT[j], at : at + 8, :] = done[r * 8 : r * 8 + 8, 0:128]
            out_ref[CTX_SLOT[j], at + 8 : at + 16, :] = done[r * 8 : r * 8 + 8, 128:256]


def gradients(recv):
    blocks, height, _ = recv.shape
    span = (height - 8) // 2
    tokens = blocks * span * 128 // 32
    rows = tokens // TILE * 32
    return pl.pallas_call(
        gradients_kernel,
        out_shape=pltpu.VMEM((blocks, span + 8, 128), jnp.bfloat16),
        in_specs=[pl.BlockSpec(memory_space=pltpu.VMEM)],
        out_specs=pl.BlockSpec(memory_space=pltpu.VMEM),
        scratch_shapes=[
            pltpu.VMEM((rows, TILE), jnp.bfloat16),
            pltpu.VMEM((2 * rows + 192, TILE), jnp.bfloat16),
            pltpu.VMEM((rows, TILE), jnp.bfloat16),
            pltpu.VMEM((TILE, tokens), jnp.bfloat16),
            pltpu.VMEM((128, tokens), jnp.float32),
            pltpu.VMEM((rows, TILE), jnp.float32),
        ],
        name="gradients",
    )(pltpu.with_memory_space_constraint(recv, pltpu.VMEM))


def spread_kernel(back_ref, out_ref):
    blocks, height, _ = back_ref.shape
    receivers, groups, own = out_ref.shape
    pieces = own // 128
    parts = [back_ref[i, height - 8 : height, :].astype(jnp.float32) for i in range(blocks)]
    parts = [x[0:pieces, :] + x[pieces : 2 * pieces, :] for x in parts]
    each = blocks // groups
    sums = [sum(parts[g * each + 1 : (g + 1) * each], parts[g * each]) for g in range(groups)]
    owned = jnp.concatenate(
        [jnp.concatenate([x[q : q + 1, :] for x in sums], axis=0) for q in range(pieces)], axis=1
    )
    for n in range(receivers):
        out_ref[n, :, :] = owned


def spread(back, receivers, groups, own):
    return pl.pallas_call(
        spread_kernel,
        out_shape=pltpu.VMEM((receivers, groups, own), jnp.float32),
        in_specs=[pl.BlockSpec(memory_space=pltpu.VMEM)],
        out_specs=pl.BlockSpec(memory_space=pltpu.VMEM),
        name="spread",
    )(back)


def finish_kernel(back_ref, mine_ref, theirs_ref, ig_ref, fg_ref, both_ref, sems):
    span = ig_ref.shape[1]
    senders, groups, own = mine_ref.shape
    copies = [pltpu.make_async_copy(back_ref.at[:, 0:span, :], ig_ref, sems.at[0])]
    copies[0].start()
    first = lax.rem(lax.axis_index("ch"), 2) == 0
    half = senders // 2
    for part in range(2):
        for n in range(part * half, (part + 1) * half):
            mine, theirs = mine_ref[n ^ FIRST_CHIP, :, :], theirs_ref[n ^ FIRST_CHIP, :, :]
            both_ref[n, 0:groups, :] = jnp.where(first, mine, theirs)
            both_ref[n, groups : 2 * groups, :] = jnp.where(first, theirs, mine)
        copy = pltpu.make_async_copy(
            both_ref.at[part * half : (part + 1) * half],
            fg_ref.at[part * half : (part + 1) * half],
            sems.at[1 + part],
        )
        copy.start()
        copies.append(copy)
    for copy in copies:
        copy.wait()


def finish(back, mine, theirs):
    senders, groups, own = mine.shape
    return pl.pallas_call(
        finish_kernel,
        out_shape=(
            jax.ShapeDtypeStruct((back.shape[0], back.shape[1] - 8, 128), jnp.bfloat16),
            jax.ShapeDtypeStruct((senders, 2 * groups, own), jnp.float32),
        ),
        in_specs=[pl.BlockSpec(memory_space=pltpu.VMEM)] * 3,
        out_specs=(pl.BlockSpec(memory_space=pl.ANY),) * 2,
        scratch_shapes=[
            pltpu.VMEM((senders, 2 * groups, own), jnp.float32),
            pltpu.SemaphoreType.DMA((3,)),
        ],
        name="finish",
    )(*(pltpu.with_memory_space_constraint(x, pltpu.VMEM) for x in (back, mine, theirs)))


def per_device(conv_input, output_grad, long_filter):
    channels, own = conv_input.shape
    cycle = lax.axis_size("ctx")
    groups_here = channels // (C // G)
    send = pack(conv_input, output_grad, long_filter, cycle)
    ring = [[p ^ FIRST_CTX for p in range(cycle)]]
    recv = lax.all_to_all(send, "ctx", 0, 0, axis_index_groups=ring, tiled=True)
    back = lax.all_to_all(gradients(recv), "ctx", 0, 0, axis_index_groups=ring, tiled=True)
    back = pltpu.with_memory_space_constraint(back, pltpu.VMEM)
    peers = lax.axis_size("ch")
    mine = lax.all_to_all(
        spread(back, peers // 2, groups_here, own),
        "ch",
        0,
        0,
        axis_index_groups=[
            [2 * (p ^ FIRST_CHIP) + core for p in range(peers // 2)] for core in range(2)
        ],
        tiled=True,
    )
    theirs = lax.ppermute(mine, "ch", [(k, k ^ 1) for k in range(peers)])
    input_grad, filter_grad = finish(back, mine, theirs)
    input_grad = input_grad.reshape(channels // 8, own // 128, 8, 128).transpose(0, 2, 1, 3)
    return input_grad.reshape(channels, own), filter_grad.reshape(G, own)


def solution(mesh):
    in_specs = (P("ch", "ctx"), P("ch", "ctx"), P(None, "ctx"))
    out_specs = (P("ch", "ctx"), P(None, "ctx"))
    return jax.shard_map(
        per_device, mesh=mesh, in_specs=in_specs, out_specs=out_specs, check_vma=False
    )
```

```python
import jax
import jax.numpy as jnp
from jax import lax
from jax.experimental import pallas as pl
from jax.experimental.pallas import tpu as pltpu
from jax.sharding import PartitionSpec as P

C = 8192
G = 128
TILE = 256
CHUNK = 512
FIRST_CTX = 6
FIRST_CHIP = 4
CTX_SLOT = [j ^ FIRST_CTX for j in range(8)]


def pack_kernel(ci_ref, og_ref, filter_ref, send_ref, taps_ref, sems):
    blocks, span, _ = ci_ref.shape
    pieces = filter_ref.shape[1] // 128
    k = lax.axis_index("ch")
    at = pl.multiple_of(8 * lax.div(k, 2), 8)
    copies = [
        pltpu.make_async_copy(filter_ref.at[pl.ds(at, 8), :], taps_ref, sems.at[0]),
        pltpu.make_async_copy(ci_ref, send_ref.at[:, 0:span, :], sems.at[1]),
        pltpu.make_async_copy(og_ref, send_ref.at[:, span : 2 * span, :], sems.at[2]),
    ]
    for copy in copies:
        copy.start()
    copies[0].wait()
    taps = taps_ref[...].astype(jnp.float32)
    taps = jnp.where(lax.rem(k, 2) == 0, taps[0:4, :], taps[4:8, :])
    for g in range(4):
        rows = [taps[g : g + 1, q * 128 : (q + 1) * 128] for q in range(pieces)]
        block = jnp.concatenate(rows + rows, axis=0).astype(jnp.bfloat16)
        for i in range(g * blocks // 4, (g + 1) * blocks // 4):
            send_ref[i, 2 * span : 2 * span + 8, :] = block
    copies[1].wait()
    copies[2].wait()


def tiles_of(x, blocks):
    channels, own = x.shape
    x = x.reshape(channels // 8, 8, own // 128, 128).transpose(0, 2, 1, 3)
    return x.reshape(blocks, channels * own // (128 * blocks), 128)


def pack(conv_input, output_grad, long_filter, blocks):
    channels, own = conv_input.shape
    span = channels * own // (128 * blocks)
    return pl.pallas_call(
        pack_kernel,
        out_shape=pltpu.VMEM((blocks, 2 * span + 8, 128), jnp.bfloat16),
        in_specs=[pl.BlockSpec(memory_space=pl.ANY)] * 3,
        out_specs=pl.BlockSpec(memory_space=pltpu.VMEM),
        scratch_shapes=[pltpu.VMEM((8, own), jnp.bfloat16), pltpu.SemaphoreType.DMA((3,))],
        name="pack",
    )(tiles_of(conv_input, blocks), tiles_of(output_grad, blocks), long_filter)


def roll_left(x, amount):
    lanes = x.shape[1]
    return x if amount == 0 else pltpu.roll(x, lanes - amount, 1)


def gradients_kernel(
    recv_ref, out_ref, og_ref, pair_ref, cit_ref, table_ref, skew_ref, acc_ref
):
    blocks, height, _ = recv_ref.shape
    per = 32
    pieces = (height - 8) // (2 * per)
    span = pieces * per
    own = pieces * 128
    tokens = blocks * own
    tiles = tokens // TILE
    rows = tiles * per
    small = tokens // 128

    def piece(base, a, r):
        j, q = divmod(a, pieces)
        at = base + (r * pieces + q) * 8
        return recv_ref[CTX_SLOT[j], at : at + 8, :]

    for a in range(small):
        for r in range(per // 8):
            x = piece(span, a, r)
            to = slice(a * per + r * 8, a * per + r * 8 + 8)
            pair_ref[to, 0:128] = x
            if a > 0:
                pair_ref[to.start - per : to.stop - per, 128:256] = x
            to = slice(a // 2 * per + r * 8, a // 2 * per + r * 8 + 8)
            og_ref[to, (a % 2) * 128 : (a % 2) * 128 + 128] = x
    pair_ref[(small - 1) * per : small * per, 128:256] = jnp.zeros((per, 128), pair_ref.dtype)
    pair_ref[small * per :, :] = jnp.zeros((pair_ref.shape[0] - small * per, TILE), pair_ref.dtype)
    for m in range(small // 8):
        ci = [piece(0, a, r) for a in range(8 * m, 8 * m + 8) for r in range(per // 8)]
        cit_ref[m * 128 : (m + 1) * 128, :] = jnp.concatenate(ci, axis=0).T

    taps = [
        recv_ref[CTX_SLOT[j], 2 * span : 2 * span + 8, :].astype(jnp.float32)
        for j in range(blocks)
    ]
    taps = jnp.concatenate([x[q : q + 1, :] for x in taps for q in range(pieces)], axis=1)
    wide = jnp.broadcast_to(taps, (8, tokens))
    base = pltpu.roll(wide, 0, 1, stride=1, stride_axis=0)
    for lo in range(0, tokens, CHUNK):
        before = (lo - 128) % tokens
        wide = jnp.concatenate([base[:, before : before + 128], base[:, lo : lo + CHUNK]], axis=1)
        for t in range(0, 16, 2):
            pair = [wide if t == 0 else pltpu.roll(wide, 8 * t, 1), pltpu.roll(wide, 8 * t + 8, 1)]
            pair = jnp.concatenate(pair, axis=0)[:, 128:]
            if lo == 0:
                u = 8 * t + lax.broadcasted_iota(jnp.int32, (16, 128), 0)
                v = lax.broadcasted_iota(jnp.int32, (16, 128), 1)
                first = jnp.where(v >= u, pair[:, 0:128], 0.0)
                pair = jnp.concatenate([first, pair[:, 128:]], axis=1)
            pair = pair.astype(jnp.bfloat16)
            row = slice(8 * t, 8 * t + 16)
            table_ref[row, lo : lo + CHUNK] = pair
            row = slice(128 + 8 * t, 128 + 8 * t + 16)
            stop = min(lo + CHUNK + 128, tokens)
            table_ref[row, lo + 128 : stop] = pair[:, : stop - lo - 128]
            if lo == 0:
                table_ref[row, 0:128] = jnp.zeros((16, 128), jnp.bfloat16)

    for n in range(tiles):
        parts = n // 4 + 1
        cross = jnp.dot(
            cit_ref[0 : parts * 128, :],
            pair_ref[n * 2 * per : n * 2 * per + 8 * per, :],
            preferred_element_type=jnp.float32,
        )
        for m in range(parts):
            term = cross[m * 128 : (m + 1) * 128, :]
            d = n - 4 * m
            if d == 0:
                u = lax.broadcasted_iota(jnp.int32, (128, TILE), 0)
                v = lax.broadcasted_iota(jnp.int32, (128, TILE), 1)
                term = jnp.where(v >= u, term, 0.0)
            to = slice(d * TILE, (d + 1) * TILE)
            skew_ref[:, to] = term if m == 0 else skew_ref[:, to] + term
    folded = []
    for lo in range(0, tokens, CHUNK):
        after = (lo + CHUNK) % tokens
        total = skew_ref[0:8, lo : lo + CHUNK]
        for t in range(1, 16):
            row = slice(8 * t, 8 * t + 8)
            wide = [skew_ref[row, lo : lo + CHUNK], skew_ref[row, after : after + 128]]
            total = total + roll_left(jnp.concatenate(wide, axis=1), 8 * t)[:, 0:CHUNK]
        folded.append(total)
    folded = jnp.concatenate(folded, axis=1)
    r = lax.broadcasted_iota(jnp.int32, folded.shape, 0)
    for bit in (1, 2, 4):
        folded = jnp.where((r & bit) > 0, roll_left(folded, bit), folded)
    lags = jnp.sum(folded, axis=0, keepdims=True)
    high = lags.astype(jnp.bfloat16).astype(jnp.float32)
    low = lags - high
    for j in range(blocks):
        packed = [
            part[:, at : at + 128]
            for part in (high, low)
            for at in range(j * own, (j + 1) * own, 128)
        ]
        out_ref[CTX_SLOT[j], span : span + 8, :] = jnp.concatenate(packed, axis=0).astype(jnp.bfloat16)

    for d in range(tiles):
        live = rows - d * per
        term = lax.dot_general(
            og_ref[d * per : rows, :],
            table_ref[:, d * TILE : (d + 1) * TILE],
            (((1,), (1,)), ((), ())),
            preferred_element_type=jnp.float32,
        )
        if d == 0:
            acc_ref[...] = term
        else:
            acc_ref[0:live, :] = acc_ref[0:live, :] + term
    for a in range(tiles):
        j, q = divmod(2 * a, pieces)
        done = acc_ref[a * per : (a + 1) * per, :].astype(jnp.bfloat16)
        for r in range(per // 8):
            at = (r * pieces + q) * 8
            out_ref[CTX_SLOT[j], at : at + 8, :] = done[r * 8 : r * 8 + 8, 0:128]
            out_ref[CTX_SLOT[j], at + 8 : at + 16, :] = done[r * 8 : r * 8 + 8, 128:256]


def gradients(recv):
    blocks, height, _ = recv.shape
    span = (height - 8) // 2
    tokens = blocks * span * 128 // 32
    rows = tokens // TILE * 32
    return pl.pallas_call(
        gradients_kernel,
        out_shape=pltpu.VMEM((blocks, span + 8, 128), jnp.bfloat16),
        in_specs=[pl.BlockSpec(memory_space=pltpu.VMEM)],
        out_specs=pl.BlockSpec(memory_space=pltpu.VMEM),
        scratch_shapes=[
            pltpu.VMEM((rows, TILE), jnp.bfloat16),
            pltpu.VMEM((2 * rows + 192, TILE), jnp.bfloat16),
            pltpu.VMEM((rows, TILE), jnp.bfloat16),
            pltpu.VMEM((TILE, tokens), jnp.bfloat16),
            pltpu.VMEM((128, tokens), jnp.float32),
            pltpu.VMEM((rows, TILE), jnp.float32),
        ],
        name="gradients",
    )(pltpu.with_memory_space_constraint(recv, pltpu.VMEM))


def spread_kernel(back_ref, out_ref):
    blocks, height, _ = back_ref.shape
    receivers, groups, own = out_ref.shape
    pieces = own // 128
    parts = [back_ref[i, height - 8 : height, :].astype(jnp.float32) for i in range(blocks)]
    parts = [x[0:pieces, :] + x[pieces : 2 * pieces, :] for x in parts]
    each = blocks // groups
    sums = [sum(parts[g * each + 1 : (g + 1) * each], parts[g * each]) for g in range(groups)]
    owned = jnp.concatenate(
        [jnp.concatenate([x[q : q + 1, :] for x in sums], axis=0) for q in range(pieces)], axis=1
    )
    for n in range(receivers):
        out_ref[n, :, :] = owned


def spread(back, receivers, groups, own):
    return pl.pallas_call(
        spread_kernel,
        out_shape=pltpu.VMEM((receivers, groups, own), jnp.float32),
        in_specs=[pl.BlockSpec(memory_space=pltpu.VMEM)],
        out_specs=pl.BlockSpec(memory_space=pltpu.VMEM),
        name="spread",
    )(back)


def finish_kernel(back_ref, mine_ref, theirs_ref, ig_ref, fg_ref, both_ref, sems):
    span = ig_ref.shape[1]
    senders, groups, own = mine_ref.shape
    copies = [pltpu.make_async_copy(back_ref.at[:, 0:span, :], ig_ref, sems.at[0])]
    copies[0].start()
    first = lax.rem(lax.axis_index("ch"), 2) == 0
    half = senders // 2
    for part in range(2):
        for n in range(part * half, (part + 1) * half):
            mine, theirs = mine_ref[n ^ FIRST_CHIP, :, :], theirs_ref[n ^ FIRST_CHIP, :, :]
            both_ref[n, 0:groups, :] = jnp.where(first, mine, theirs)
            both_ref[n, groups : 2 * groups, :] = jnp.where(first, theirs, mine)
        copy = pltpu.make_async_copy(
            both_ref.at[part * half : (part + 1) * half],
            fg_ref.at[part * half : (part + 1) * half],
            sems.at[1 + part],
        )
        copy.start()
        copies.append(copy)
    for copy in copies:
        copy.wait()


def finish(back, mine, theirs):
    senders, groups, own = mine.shape
    return pl.pallas_call(
        finish_kernel,
        out_shape=(
            jax.ShapeDtypeStruct((back.shape[0], back.shape[1] - 8, 128), jnp.bfloat16),
            jax.ShapeDtypeStruct((senders, 2 * groups, own), jnp.float32),
        ),
        in_specs=[pl.BlockSpec(memory_space=pltpu.VMEM)] * 3,
        out_specs=(pl.BlockSpec(memory_space=pl.ANY),) * 2,
        scratch_shapes=[
            pltpu.VMEM((senders, 2 * groups, own), jnp.float32),
            pltpu.SemaphoreType.DMA((3,)),
        ],
        name="finish",
    )(*(pltpu.with_memory_space_constraint(x, pltpu.VMEM) for x in (back, mine, theirs)))


def per_device(conv_input, output_grad, long_filter):
    channels, own = conv_input.shape
    cycle = lax.axis_size("ctx")
    groups_here = channels // (C // G)
    send = pack(conv_input, output_grad, long_filter, cycle)
    ring = [[p ^ FIRST_CTX for p in range(cycle)]]
    recv = lax.all_to_all(send, "ctx", 0, 0, axis_index_groups=ring, tiled=True)
    back = lax.all_to_all(gradients(recv), "ctx", 0, 0, axis_index_groups=ring, tiled=True)
    back = pltpu.with_memory_space_constraint(back, pltpu.VMEM)
    peers = lax.axis_size("ch")
    mine = lax.all_to_all(
        spread(back, peers // 2, groups_here, own),
        "ch",
        0,
        0,
        axis_index_groups=[
            [2 * (p ^ FIRST_CHIP) + core for p in range(peers // 2)] for core in range(2)
        ],
        tiled=True,
    )
    theirs = lax.ppermute(mine, "ch", [(k, k ^ 1) for k in range(peers)])
    input_grad, filter_grad = finish(back, mine, theirs)
    input_grad = input_grad.reshape(channels // 8, own // 128, 8, 128).transpose(0, 2, 1, 3)
    return input_grad.reshape(channels, own), filter_grad.reshape(G, own)


def solution(mesh):
    in_specs = (P("ch", "ctx"), P("ch", "ctx"), P(None, "ctx"))
    out_specs = (P("ch", "ctx"), P(None, "ctx"))
    return jax.shard_map(
        per_device, mesh=mesh, in_specs=in_specs, out_specs=out_specs, check_vma=False
    )
```

```python
import jax
import jax.numpy as jnp
from jax import lax
from jax.experimental import pallas as pl
from jax.experimental.pallas import tpu as pltpu
from jax.sharding import PartitionSpec as P

C = 8192
G = 128
TILE = 256
CHUNK = 512
FIRST_CTX = 6
FIRST_CHIP = 4
CTX_SLOT = [j ^ FIRST_CTX for j in range(8)]


def pack_kernel(ci_ref, og_ref, filter_ref, send_ref, taps_ref, sems):
    blocks, span, _ = ci_ref.shape
    pieces = filter_ref.shape[1] // 128
    k = lax.axis_index("ch")
    at = pl.multiple_of(8 * lax.div(k, 2), 8)
    copies = [
        pltpu.make_async_copy(filter_ref.at[pl.ds(at, 8), :], taps_ref, sems.at[0]),
        pltpu.make_async_copy(ci_ref, send_ref.at[:, 0:span, :], sems.at[1]),
        pltpu.make_async_copy(og_ref, send_ref.at[:, span : 2 * span, :], sems.at[2]),
    ]
    for copy in copies:
        copy.start()
    copies[0].wait()
    taps = taps_ref[...].astype(jnp.float32)
    taps = jnp.where(lax.rem(k, 2) == 0, taps[0:4, :], taps[4:8, :])
    for g in range(4):
        rows = [taps[g : g + 1, q * 128 : (q + 1) * 128] for q in range(pieces)]
        block = jnp.concatenate(rows + rows, axis=0).astype(jnp.bfloat16)
        for i in range(g * blocks // 4, (g + 1) * blocks // 4):
            send_ref[i, 2 * span : 2 * span + 8, :] = block
    copies[1].wait()
    copies[2].wait()


def tiles_of(x, blocks):
    channels, own = x.shape
    x = x.reshape(channels // 8, 8, own // 128, 128).transpose(0, 2, 1, 3)
    return x.reshape(blocks, channels * own // (128 * blocks), 128)


def pack(conv_input, output_grad, long_filter, blocks):
    channels, own = conv_input.shape
    span = channels * own // (128 * blocks)
    return pl.pallas_call(
        pack_kernel,
        out_shape=pltpu.VMEM((blocks, 2 * span + 8, 128), jnp.bfloat16),
        in_specs=[pl.BlockSpec(memory_space=pl.ANY)] * 3,
        out_specs=pl.BlockSpec(memory_space=pltpu.VMEM),
        scratch_shapes=[pltpu.VMEM((8, own), jnp.bfloat16), pltpu.SemaphoreType.DMA((3,))],
        name="pack",
    )(tiles_of(conv_input, blocks), tiles_of(output_grad, blocks), long_filter)


def roll_left(x, amount):
    lanes = x.shape[1]
    return x if amount == 0 else pltpu.roll(x, lanes - amount, 1)


def gradients_kernel(
    recv_ref, out_ref, og_ref, pair_ref, cit_ref, table_ref, skew_ref, acc_ref
):
    blocks, height, _ = recv_ref.shape
    per = 32
    pieces = (height - 8) // (2 * per)
    span = pieces * per
    own = pieces * 128
    tokens = blocks * own
    tiles = tokens // TILE
    rows = tiles * per
    small = tokens // 128

    def piece(base, a, r):
        j, q = divmod(a, pieces)
        at = base + (r * pieces + q) * 8
        return recv_ref[CTX_SLOT[j], at : at + 8, :]

    for a in range(small):
        for r in range(per // 8):
            x = piece(span, a, r)
            to = slice(a * per + r * 8, a * per + r * 8 + 8)
            pair_ref[to, 0:128] = x
            if a > 0:
                pair_ref[to.start - per : to.stop - per, 128:256] = x
            to = slice(a // 2 * per + r * 8, a // 2 * per + r * 8 + 8)
            og_ref[to, (a % 2) * 128 : (a % 2) * 128 + 128] = x
    pair_ref[(small - 1) * per : small * per, 128:256] = jnp.zeros((per, 128), pair_ref.dtype)
    pair_ref[small * per :, :] = jnp.zeros((pair_ref.shape[0] - small * per, TILE), pair_ref.dtype)
    for m in range(small // 8):
        ci = [piece(0, a, r) for a in range(8 * m, 8 * m + 8) for r in range(per // 8)]
        cit_ref[m * 128 : (m + 1) * 128, :] = jnp.concatenate(ci, axis=0).T

    taps = [
        recv_ref[CTX_SLOT[j], 2 * span : 2 * span + 8, :].astype(jnp.float32)
        for j in range(blocks)
    ]
    taps = jnp.concatenate([x[q : q + 1, :] for x in taps for q in range(pieces)], axis=1)
    wide = jnp.broadcast_to(taps, (8, tokens))
    base = pltpu.roll(wide, 0, 1, stride=1, stride_axis=0)
    for lo in range(0, tokens, CHUNK):
        before = (lo - 128) % tokens
        wide = jnp.concatenate([base[:, before : before + 128], base[:, lo : lo + CHUNK]], axis=1)
        for t in range(0, 16, 2):
            pair = [wide if t == 0 else pltpu.roll(wide, 8 * t, 1), pltpu.roll(wide, 8 * t + 8, 1)]
            pair = jnp.concatenate(pair, axis=0)[:, 128:]
            if lo == 0:
                u = 8 * t + lax.broadcasted_iota(jnp.int32, (16, 128), 0)
                v = lax.broadcasted_iota(jnp.int32, (16, 128), 1)
                first = jnp.where(v >= u, pair[:, 0:128], 0.0)
                pair = jnp.concatenate([first, pair[:, 128:]], axis=1)
            pair = pair.astype(jnp.bfloat16)
            row = slice(8 * t, 8 * t + 16)
            table_ref[row, lo : lo + CHUNK] = pair
            row = slice(128 + 8 * t, 128 + 8 * t + 16)
            stop = min(lo + CHUNK + 128, tokens)
            table_ref[row, lo + 128 : stop] = pair[:, : stop - lo - 128]
            if lo == 0:
                table_ref[row, 0:128] = jnp.zeros((16, 128), jnp.bfloat16)

    for n in range(tiles):
        parts = n // 4 + 1
        cross = jnp.dot(
            cit_ref[0 : parts * 128, :],
            pair_ref[n * 2 * per : n * 2 * per + 8 * per, :],
            preferred_element_type=jnp.float32,
        )
        for m in range(parts):
            term = cross[m * 128 : (m + 1) * 128, :]
            d = n - 4 * m
            if d == 0:
                u = lax.broadcasted_iota(jnp.int32, (128, TILE), 0)
                v = lax.broadcasted_iota(jnp.int32, (128, TILE), 1)
                term = jnp.where(v >= u, term, 0.0)
            to = slice(d * TILE, (d + 1) * TILE)
            skew_ref[:, to] = term if m == 0 else skew_ref[:, to] + term
    folded = []
    for lo in range(0, tokens, CHUNK):
        after = (lo + CHUNK) % tokens
        total = skew_ref[0:8, lo : lo + CHUNK]
        for t in range(1, 16):
            row = slice(8 * t, 8 * t + 8)
            wide = [skew_ref[row, lo : lo + CHUNK], skew_ref[row, after : after + 128]]
            total = total + roll_left(jnp.concatenate(wide, axis=1), 8 * t)[:, 0:CHUNK]
        folded.append(total)
    folded = jnp.concatenate(folded, axis=1)
    r = lax.broadcasted_iota(jnp.int32, folded.shape, 0)
    for bit in (1, 2, 4):
        folded = jnp.where((r & bit) > 0, roll_left(folded, bit), folded)
    lags = jnp.sum(folded, axis=0, keepdims=True)
    high = lags.astype(jnp.bfloat16).astype(jnp.float32)
    low = lags - high
    for j in range(blocks):
        packed = [
            part[:, at : at + 128]
            for part in (high, low)
            for at in range(j * own, (j + 1) * own, 128)
        ]
        out_ref[CTX_SLOT[j], span : span + 8, :] = jnp.concatenate(packed, axis=0).astype(jnp.bfloat16)

    for d in range(tiles):
        live = rows - d * per
        term = lax.dot_general(
            og_ref[d * per : rows, :],
            table_ref[:, d * TILE : (d + 1) * TILE],
            (((1,), (1,)), ((), ())),
            preferred_element_type=jnp.float32,
        )
        if d == 0:
            acc_ref[...] = term
        else:
            acc_ref[0:live, :] = acc_ref[0:live, :] + term
        a = tiles - 1 - d
        j, q = divmod(2 * a, pieces)
        done = acc_ref[a * per : (a + 1) * per, :].astype(jnp.bfloat16)
        for r in range(per // 8):
            at = (r * pieces + q) * 8
            out_ref[CTX_SLOT[j], at : at + 8, :] = done[r * 8 : r * 8 + 8, 0:128]
            out_ref[CTX_SLOT[j], at + 8 : at + 16, :] = done[r * 8 : r * 8 + 8, 128:256]


def gradients(recv):
    blocks, height, _ = recv.shape
    span = (height - 8) // 2
    tokens = blocks * span * 128 // 32
    rows = tokens // TILE * 32
    return pl.pallas_call(
        gradients_kernel,
        out_shape=pltpu.VMEM((blocks, span + 8, 128), jnp.bfloat16),
        in_specs=[pl.BlockSpec(memory_space=pltpu.VMEM)],
        out_specs=pl.BlockSpec(memory_space=pltpu.VMEM),
        scratch_shapes=[
            pltpu.VMEM((rows, TILE), jnp.bfloat16),
            pltpu.VMEM((2 * rows + 192, TILE), jnp.bfloat16),
            pltpu.VMEM((rows, TILE), jnp.bfloat16),
            pltpu.VMEM((TILE, tokens), jnp.bfloat16),
            pltpu.VMEM((128, tokens), jnp.float32),
            pltpu.VMEM((rows, TILE), jnp.float32),
        ],
        name="gradients",
    )(pltpu.with_memory_space_constraint(recv, pltpu.VMEM))


def spread_kernel(back_ref, out_ref):
    blocks, height, _ = back_ref.shape
    receivers, groups, own = out_ref.shape
    pieces = own // 128
    parts = [back_ref[i, height - 8 : height, :].astype(jnp.float32) for i in range(blocks)]
    parts = [x[0:pieces, :] + x[pieces : 2 * pieces, :] for x in parts]
    each = blocks // groups
    sums = [sum(parts[g * each + 1 : (g + 1) * each], parts[g * each]) for g in range(groups)]
    owned = jnp.concatenate(
        [jnp.concatenate([x[q : q + 1, :] for x in sums], axis=0) for q in range(pieces)], axis=1
    )
    for n in range(receivers):
        out_ref[n, :, :] = owned


def spread(back, receivers, groups, own):
    return pl.pallas_call(
        spread_kernel,
        out_shape=pltpu.VMEM((receivers, groups, own), jnp.float32),
        in_specs=[pl.BlockSpec(memory_space=pltpu.VMEM)],
        out_specs=pl.BlockSpec(memory_space=pltpu.VMEM),
        name="spread",
    )(back)


def finish_kernel(back_ref, mine_ref, theirs_ref, ig_ref, fg_ref, both_ref, sems):
    span = ig_ref.shape[1]
    senders, groups, own = mine_ref.shape
    copies = [pltpu.make_async_copy(back_ref.at[:, 0:span, :], ig_ref, sems.at[0])]
    copies[0].start()
    first = lax.rem(lax.axis_index("ch"), 2) == 0
    half = senders // 2
    for part in range(2):
        for n in range(part * half, (part + 1) * half):
            mine, theirs = mine_ref[n ^ FIRST_CHIP, :, :], theirs_ref[n ^ FIRST_CHIP, :, :]
            both_ref[n, 0:groups, :] = jnp.where(first, mine, theirs)
            both_ref[n, groups : 2 * groups, :] = jnp.where(first, theirs, mine)
        copy = pltpu.make_async_copy(
            both_ref.at[part * half : (part + 1) * half],
            fg_ref.at[part * half : (part + 1) * half],
            sems.at[1 + part],
        )
        copy.start()
        copies.append(copy)
    for copy in copies:
        copy.wait()


def finish(back, mine, theirs):
    senders, groups, own = mine.shape
    return pl.pallas_call(
        finish_kernel,
        out_shape=(
            jax.ShapeDtypeStruct((back.shape[0], back.shape[1] - 8, 128), jnp.bfloat16),
            jax.ShapeDtypeStruct((senders, 2 * groups, own), jnp.float32),
        ),
        in_specs=[pl.BlockSpec(memory_space=pltpu.VMEM)] * 3,
        out_specs=(pl.BlockSpec(memory_space=pl.ANY),) * 2,
        scratch_shapes=[
            pltpu.VMEM((senders, 2 * groups, own), jnp.float32),
            pltpu.SemaphoreType.DMA((3,)),
        ],
        name="finish",
    )(*(pltpu.with_memory_space_constraint(x, pltpu.VMEM) for x in (back, mine, theirs)))


def per_device(conv_input, output_grad, long_filter):
    channels, own = conv_input.shape
    cycle = lax.axis_size("ctx")
    groups_here = channels // (C // G)
    send = pack(conv_input, output_grad, long_filter, cycle)
    ring = [[p ^ FIRST_CTX for p in range(cycle)]]
    recv = lax.all_to_all(send, "ctx", 0, 0, axis_index_groups=ring, tiled=True)
    back = lax.all_to_all(gradients(recv), "ctx", 0, 0, axis_index_groups=ring, tiled=True)
    back = pltpu.with_memory_space_constraint(back, pltpu.VMEM)
    peers = lax.axis_size("ch")
    mine = lax.all_to_all(
        spread(back, peers // 2, groups_here, own),
        "ch",
        0,
        0,
        axis_index_groups=[
            [2 * (p ^ FIRST_CHIP) + core for p in range(peers // 2)] for core in range(2)
        ],
        tiled=True,
    )
    theirs = lax.ppermute(mine, "ch", [(k, k ^ 1) for k in range(peers)])
    input_grad, filter_grad = finish(back, mine, theirs)
    input_grad = input_grad.reshape(channels // 8, own // 128, 8, 128).transpose(0, 2, 1, 3)
    return input_grad.reshape(channels, own), filter_grad.reshape(G, own)


def solution(mesh):
    in_specs = (P("ch", "ctx"), P("ch", "ctx"), P(None, "ctx"))
    out_specs = (P("ch", "ctx"), P(None, "ctx"))
    return jax.shard_map(
        per_device, mesh=mesh, in_specs=in_specs, out_specs=out_specs, check_vma=False
    )
```
